32 devices in a mesh: branch: 8 (over y, x, core), mode: 4 (over z).
Axes of the slice: x: 2, y: 2, z: 4, core: 2. Of those that a mesh axis runs over, the one named last changes fastest.
Arguments:
- stem: float32 [2, 8, 512, 4, 512], P(None, 'branch', None, 'mode'), may hold values from -6 to 6
- left_factors: bfloat16 [2, 2, 8, 512, 512], P(None, None, 'branch', 'mode'), may hold values from -0.1875 to 0.1875
- right_factors: bfloat16 [2, 2, 8, 512, 512], P(None, None, 'branch', 'mode'), may hold values from -0.1875 to 0.1875
- owners: int32 [2], replicated, may hold values from 0 to 7
Outputs:
- contracted: float32 [2, 8, 512, 4, 512], P(None, 'branch', None, 'mode')
The draws below stay inside these ranges and needn't reach their ends.
All inputs are finite; a program needn't handle non-finite values.
Results may differ from the reference program's by a relative error of at most 0.0003.
Values may be sent and summed in bfloat16 or wider, within the bound.
No kernel may reach another device: no remote copies, remote signals or barrier semaphores. Data moves between devices by JAX's collectives and lax.ppermute only.
A program may use at most 64 MiB of HBM per device.

```python
import jax
import jax.numpy as jnp
from jax import lax

WIDTH = 512
ROWS = 512
SLICES = 8
SPREAD = 4
N_BRANCH = 8


def levels(rng, dims, pieces, low, high):
    factor_of = 1.0
    for position, blocks in pieces:
        steps = jax.random.uniform(jax.random.fold_in(jax.random.fold_in(rng, 6), position), (blocks,), jnp.float32, low / len(pieces), high / len(pieces))
        factor_of = factor_of * jnp.repeat(jnp.exp(steps), dims[position] // blocks).reshape((-1,) + (1,) * (len(dims) - 1 - position))
    return factor_of


def gaussian(stream_key, extent, scale, bound, pieces=(), held_as=jnp.bfloat16):
    entries = jax.random.normal(stream_key, extent, jnp.float32) * scale
    if len(pieces) > 0:
        entries = levels(stream_key, extent, pieces, -0.22, 0.18) * entries
    return jnp.clip(entries, min=-bound, max=bound).astype(held_as)


def setup_inputs(seed: int = 0) -> dict:
    streams_of = jax.random.split(jax.random.key(seed), 5)
    stem = gaussian(streams_of[0], (2, SLICES, ROWS, SPREAD, WIDTH), 1.0, 6.0, ((1, 8), (3, 4)), jnp.float32)
    left_factors = gaussian(streams_of[1], (2, 2, SLICES, WIDTH, WIDTH), (2 * WIDTH) ** -0.5, 0.1875, ((2, 8), (3, 4)))
    right_factors = gaussian(streams_of[2], (2, 2, SLICES, WIDTH, WIDTH), (2 * WIDTH) ** -0.5, 0.1875, ((2, 8), (3, 4)))
    owners = jax.random.randint(streams_of[3], (2,), 0, N_BRANCH).astype(jnp.int32)
    return {"stem": stem, "left_factors": left_factors, "right_factors": right_factors, "owners": owners}


def form_branch(left_factors, right_factors, owners, which):
    left = lax.dynamic_index_in_dim(left_factors[which], owners[which], 1, keepdims=False)
    right = lax.dynamic_index_in_dim(right_factors[which], owners[which], 1, keepdims=False)
    real_part = jnp.dot(left[0], right[0], preferred_element_type=jnp.float32) - jnp.dot(left[1], right[1], preferred_element_type=jnp.float32)
    imag_part = jnp.dot(left[0], right[1], preferred_element_type=jnp.float32) + jnp.dot(left[1], right[0], preferred_element_type=jnp.float32)
    return real_part, imag_part


def complex_apply(field_re, field_im, branch):
    high = lax.Precision.HIGHEST
    real_part = jnp.dot(field_re, branch[0], precision=high) - jnp.dot(field_im, branch[1], precision=high)
    imag_part = jnp.dot(field_re, branch[1], precision=high) + jnp.dot(field_im, branch[0], precision=high)
    return real_part, imag_part


def reference(stem, left_factors, right_factors, owners):
    first_branch = form_branch(left_factors, right_factors, owners, 0)
    second_branch = form_branch(left_factors, right_factors, owners, 1)
    spread = stem.shape[3]
    width = stem.shape[4]
    rows = stem.shape[2]

    def one_slice(piece):
        flat = piece.reshape(2, rows * spread, width)
        real_part, imag_part = complex_apply(flat[0], flat[1], first_branch)
        first = jnp.stack([real_part, imag_part]).reshape(2, rows, spread, spread, width // spread)
        swapped = jnp.swapaxes(first, 2, 3).reshape(2, rows * spread, width)
        real_two, imag_two = complex_apply(swapped[0], swapped[1], second_branch)
        return jnp.stack([real_two, imag_two]).reshape(2, rows, spread, width)

    result = lax.map(one_slice, jnp.moveaxis(stem, 1, 0))
    return jnp.moveaxis(result, 0, 1)
```

```python
import functools

import jax
import jax.numpy as jnp
from jax import lax
from jax.experimental import pallas as pl
from jax.experimental.pallas import tpu as pltpu
from jax.sharding import PartitionSpec as P


LANES = 128
NOTE = 16
TOP = 7.8
FLOOR, TINY = 1e-20, 2.0**-126
F32, BF16 = jnp.float32, jnp.bfloat16
VMEM = pl.BlockSpec(memory_space=pltpu.VMEM)
SMEM = pl.BlockSpec(memory_space=pltpu.SMEM)


def swap(value, axis, mask):
    size = lax.axis_size(axis)
    return lax.ppermute(value, axis, [(i, i ^ mask) for i in range(size)])


def halves(value):
    high = value.astype(BF16)
    return high, (value - high.astype(F32)).astype(BF16)


def matmul(a, b):
    return jnp.dot(a, b, preferred_element_type=F32)


def product(high, low, right_high, right_low):
    return matmul(high, right_high) + matmul(low, right_high) + matmul(high, right_low)


def call(body, outs, *, flops, moved, limit=24 << 20, scratch=(), ins):
    return pl.pallas_call(
        body,
        out_shape=outs,
        in_specs=ins,
        out_specs=jax.tree.map(lambda _: VMEM, outs),
        scratch_shapes=scratch,
        compiler_params=pltpu.CompilerParams(vmem_limit_bytes=limit),
        cost_estimate=pl.CostEstimate(flops=flops, bytes_accessed=moved, transcendentals=0),
    )


def spread(both, owner):
    nb = lax.axis_size("branch")
    chips = nb // 2
    here = lax.axis_index("branch")
    core, chip = here % 2, here // 2
    side, parts, rows, width = both.shape
    cut = rows // nb
    pieces = both.reshape(side, parts, 2, chips, cut, width)
    keep = lax.dynamic_index_in_dim(pieces, core, 2, keepdims=False)
    give = lax.dynamic_index_in_dim(pieces, 1 - core, 2, keepdims=False)
    got = swap(give, "branch", 1)
    half = jnp.where(core == owner % 2, keep, got)
    piece = lax.dynamic_index_in_dim(half, chip, 2, keepdims=False)
    for mask in range(1, chips):
        sent = lax.dynamic_index_in_dim(half, chip ^ mask, 2, keepdims=False)
        came = swap(sent, "branch", 2 * mask)
        piece = jnp.where(owner // 2 == chip ^ mask, came, piece)
    layers = lax.all_gather(piece, "mode", axis=0)
    blocks = []
    for mask in range(chips):
        mine = swap(layers, "branch", 2 * mask) if mask else layers
        blocks.append(mine)
        blocks.append(swap(mine, "branch", 1))
    return blocks


def place(pos, blocks, store):
    core, chip = pos[0], pos[1]
    for index, block in enumerate(blocks):
        mask, other = index // 2, index % 2
        layers, _, _, cut, _ = block.shape
        side = 1 - core if other else core
        for layer in range(layers):
            per = len(blocks) * cut
            row = layer * per + side * (per // 2) + (chip ^ mask) * cut
            store(layer, block, pl.multiple_of(row, cut), cut)


def split_kernel(stem, high, low):
    parts, count, _ = stem.shape
    rows = high.shape[0]
    steps = count // rows
    for part in range(parts):
        for step in range(steps):
            value = stem[part, pl.ds(step, rows, stride=steps), :]
            columns = pl.ds((part * steps + step) * LANES, LANES)
            high[:, columns], low[:, columns] = halves(value)


def weights(re, im):
    return jnp.concatenate(
        [jnp.concatenate([re, im], axis=1), jnp.concatenate([-im, re], axis=1)], axis=0
    )


def encode(value, out):
    rows, columns = value.shape
    peak = jnp.max(jnp.abs(value), axis=0, keepdims=True)
    scale = (jnp.maximum(peak, FLOOR) * 2.0**-TOP).astype(BF16)
    power = value * (1.0 / scale.astype(F32))
    sign = jnp.where(power < 0.0, -1.0, 1.0)
    for _ in range(4):
        power = power * power
    out[pl.ds(0, rows), :] = (sign * power).astype(BF16)
    out[pl.ds(rows, NOTE), :] = jnp.broadcast_to(scale, (NOTE, columns))


def first_kernel(targets, pos, high, low, *refs):
    n = len(refs) - len(targets) - 4
    blocks, outs = refs[:n], refs[n : n + len(targets)]
    left, right, w_high, w_low = refs[n + len(targets) :]
    width = left.shape[0]

    def store_left(layer, block, row, cut):
        for part in range(2):
            left[pl.ds(row, cut), pl.ds(part * width, width)] = block[layer, 0, part]

    place(pos, blocks, store_left)
    span = outs[0].shape[1] // 2
    for target, out in zip(targets, outs):
        column = pl.multiple_of((pos[2] ^ target) * span, span)

        def store_right(layer, block, row, cut):
            for part in range(2):
                right[part, pl.ds(row, cut), :] = block[layer, 1, part, :, pl.ds(column, span)]

        place(pos, blocks, store_right)
        formed = matmul(left[...], weights(right[0], right[1]))
        w_high[...], w_low[...] = halves(weights(formed[:, :span], formed[:, span:]))
        value = product(high[...], low[...], w_high[...], w_low[...])
        if target:
            encode(value, out)
        else:
            out[...] = value


def second_branch_kernel(pos, *refs):
    blocks, (w_high, w_low, left, right) = refs[:-4], refs[-4:]
    width = left.shape[0]

    def store(layer, block, row, cut):
        for part in range(2):
            left[pl.ds(row, cut), pl.ds(part * width, width)] = block[layer, 0, part]
        re, im = block[layer, 1, 0], block[layer, 1, 1]
        right[pl.ds(row, cut), pl.ds(0, width)] = re
        right[pl.ds(row, cut), pl.ds(width, width)] = im
        right[pl.ds(row + width, cut), pl.ds(0, width)] = -im
        right[pl.ds(row + width, cut), pl.ds(width, width)] = re

    place(pos, blocks, store)
    sources, twice, _ = w_high.shape
    span = twice // 2
    for source in range(sources):
        formed = matmul(left[pl.ds(source * span, span), :], right[...])
        w_high[source], w_low[source] = halves(weights(formed[:, :width], formed[:, width:]))


def decode(block, rows):
    power = block[pl.ds(0, rows), :].astype(F32)
    scale = block[pl.ds(rows, NOTE), :][0:1].astype(F32)
    root = jnp.maximum(jnp.abs(power), TINY)
    for _ in range(4):
        root = lax.rsqrt(root)
    root = jnp.where(power < 0.0, -root, jnp.where(power > 0.0, root, 0.0))
    return root * scale


def second_kernel(masks, last, pos, w_high, w_low, *refs):
    n = len(masks)
    blocks, out = refs[:n], refs[-1]
    rows = blocks[-1].shape[0] - NOTE
    total = refs[n][...] if last else None
    for mask, block in zip(masks, blocks):
        source = pos[2] ^ mask
        term = product(*halves(decode(block, rows) if mask else block[...]), w_high[source], w_low[source])
        total = term if total is None else total + term
    if not last:
        out[...] = total
        return
    parts, count, _ = out.shape
    steps = count // rows
    for part in range(parts):
        for step in range(steps):
            column = (part * steps + step) * LANES
            out[part, pl.ds(step, rows, stride=steps), :] = total[:, column : column + LANES]


def plain(stem, pieces):
    nb = lax.axis_size("branch")
    here = lax.axis_index("branch")
    width = stem.shape[4]

    def branch(which):
        blocks = jnp.stack(pieces(which))
        blocks = blocks.reshape((nb // 2, 2) + blocks.shape[1:])
        blocks = jnp.take(blocks, (here // 2) ^ jnp.arange(nb // 2), axis=0)
        blocks = jnp.take(blocks, (here % 2) ^ jnp.arange(2), axis=1)
        left, right = blocks.transpose(3, 4, 2, 1, 0, 5, 6).reshape(2, 2, width, width)
        return (
            matmul(left[0], right[0]) - matmul(left[1], right[1]),
            matmul(left[0], right[1]) + matmul(left[1], right[0]),
        )

    def apply(field, branch):
        dot = functools.partial(jnp.dot, precision=lax.Precision.HIGHEST)
        return jnp.stack(
            [
                dot(field[0], branch[0]) - dot(field[1], branch[1]),
                dot(field[0], branch[1]) + dot(field[1], branch[0]),
            ]
        )

    first = apply(stem[:, 0, :, 0, :], branch(0))
    moved = lax.all_to_all(first[:, :, None, :], "mode", split_axis=3, concat_axis=2, tiled=True)
    return apply(moved.reshape(2, -1, width), branch(1)).reshape(stem.shape)


def shards(stem, left_factors, right_factors, owners):
    nb, nm = lax.axis_size("branch"), lax.axis_size("mode")
    rows, width = stem.shape[2], stem.shape[4]
    span = width // nm
    here, layer = lax.axis_index("branch"), lax.axis_index("mode")
    pos = jnp.stack([here % 2, here // 2, layer]).astype(jnp.int32)

    def pieces(which):
        both = jnp.stack([left_factors[which, :, 0], right_factors[which, :, 0]])
        return spread(both, owners[which])

    if span % LANES or rows % 8 or left_factors.shape[3] % (8 * nb):
        return plain(stem, pieces)

    def shape(dims, dtype):
        return jax.ShapeDtypeStruct(dims, dtype)

    one = 2 * rows * 2 * width * 2 * width
    flat = stem.reshape(2, rows * (width // LANES), LANES)
    high, low = call(
        split_kernel,
        [shape((rows, 2 * width), BF16)] * 2,
        flops=rows * width,
        moved=2 * flat.size * 4,
        ins=[VMEM],
    )(flat)

    first = pieces(0)


    def contract(targets):
        share = len(targets) * one // nm
        return call(
            functools.partial(first_kernel, targets),
            [
                shape((rows + NOTE, 2 * span), BF16) if t else shape((rows, 2 * span), F32)
                for t in targets
            ],
            flops=4 * share,
            moved=2 * flat.size * 4,
            scratch=[
                pltpu.VMEM((width, 2 * width), BF16),
                pltpu.VMEM((2, width, span), BF16),
                pltpu.VMEM((2 * width, 2 * span), BF16),
                pltpu.VMEM((2 * width, 2 * span), BF16),
            ],
            ins=[SMEM, VMEM, VMEM] + [VMEM] * len(first),
        )(pos, high, low, *first)

    order = [1] + list(range(nm - 1, 1, -1))
    came = {}
    for mask in order:
        (block,) = contract([mask])
        came[mask] = swap(block, "mode", mask)
    (came[0],) = contract([0])

    second = pieces(1)
    w_high, w_low = call(
        second_branch_kernel,
        [shape((nm, 2 * span, 2 * width), BF16)] * 2,
        flops=one,
        moved=6 * width * width * 4,
        scratch=[
            pltpu.VMEM((width, 2 * width), BF16),
            pltpu.VMEM((2 * width, 2 * width), BF16),
        ],
        ins=[SMEM] + [VMEM] * len(second),
    )(pos, *second)

    early, late = [0] + order[:-1], order[-1:]
    total = call(
        functools.partial(second_kernel, early, False),
        shape((rows, 2 * width), F32),
        flops=3 * one * len(early) // nm,
        moved=rows * width * 16,
        ins=[SMEM] + [VMEM] * (2 + len(early)),
    )(pos, w_high, w_low, *[came[m] for m in early])
    result = call(
        functools.partial(second_kernel, late, True),
        shape(flat.shape, F32),
        flops=3 * one * len(late) // nm,
        moved=rows * width * 24,
        ins=[SMEM] + [VMEM] * (3 + len(late)),
    )(pos, w_high, w_low, *[came[m] for m in late], total)
    return result.reshape(stem.shape)


def solution(mesh):
    placed = (
        P(None, "branch", None, "mode", None),
        P(None, None, "branch", "mode", None),
        P(None, None, "branch", "mode", None),
        P(),
    )
    return jax.shard_map(
        shards,
        mesh=mesh,
        in_specs=placed,
        out_specs=P(None, "branch", None, "mode", None),
        check_vma=False,
    )
```
